32 devices in a mesh: box: 8 (over y, x, core), sub: 4 (over z).
Axes of the slice: x: 2, y: 2, z: 4, core: 2. Of those that a mesh axis runs over, the one named last changes fastest.
Arguments:
- fine_state: float32 [8, 5, 8, 4096], P('box', None, 'sub'), as said below
- coarse_state: float32 [5, 4, 256, 128], P(None, 'sub', 'box'), as said below
- box_y: int32 [8], P('box'), may hold values from 1 to 95
Outputs:
- fine_next: float32 [8, 5, 8, 4096], P('box', None, 'sub')
- coarse_next: float32 [5, 4, 256, 128], P(None, 'sub', 'box')
The draws below stay inside these ranges and needn't reach their ends.
Inputs may be any that keep to these rules, and one draw needn't show every extreme that they name: `fine_state`: density and pressure of every cell are positive. `coarse_state`: density and pressure of every cell are positive.
All inputs are finite; a program needn't handle non-finite values.
Results may differ from the reference program's by a relative error of at most 0.00002.
Values sent between devices are 32-bit elements; how exact they have to be, the bound alone decides.
A program may use at most 64 MiB of HBM per device.

```python
import jax
import jax.numpy as jnp
from jax import lax

BOX = 64
LAYERS = 8
HALF = 32
CZ = 4
CX = 32
NYC = 128
BOXES = 8
COARSE_X = 256


def euler_cells(key, shape, axis):
    keys = jax.random.split(key, 3)
    density = jnp.exp(jax.random.uniform(keys[0], shape, jnp.float32, jnp.log(0.5), jnp.log(2.0)))
    velocity = 0.5 * jax.random.normal(keys[1], (3,) + shape, jnp.float32)
    pressure = jnp.exp(jax.random.uniform(keys[2], shape, jnp.float32, jnp.log(0.5), jnp.log(2.0)))
    energy = pressure / 0.4 + 0.5 * density * jnp.sum(velocity * velocity, axis=0)
    parts = [density, density * velocity[0], density * velocity[1], density * velocity[2], energy]
    return jnp.stack(parts, axis=axis)


def draw_fine_state(key, part):
    return euler_cells(jax.random.fold_in(key, 11), (BOXES, LAYERS, BOX * BOX), 1)


def draw_coarse_state(key, part):
    return euler_cells(jax.random.fold_in(key, 23), (CZ, COARSE_X, NYC), 0)


def draw_box_y(key, part):
    spread = (NYC - HALF - 1) // 2
    keys = jax.random.split(jax.random.fold_in(key, 37), 2)
    lower = jax.random.randint(keys[0], (BOXES,), 1, 1 + spread, jnp.int32)
    upper = jax.random.randint(keys[1], (BOXES,), NYC - HALF - spread, NYC - HALF, jnp.int32)
    index = jnp.arange(BOXES, dtype=jnp.int32)
    values = jnp.where(index % 2 == 0, lower, upper)
    values = jnp.where(index == 0, jnp.int32(1), values)
    values = jnp.where(index == 1, jnp.int32(NYC - HALF - 1), values)
    return values.astype(jnp.int32)


def setup_inputs(seed: int = 0) -> dict:
    splits = jax.random.split(jax.random.key(seed), 4)
    return {
        "fine_state": draw_fine_state(jax.random.fold_in(splits[3], 71), 0),
        "coarse_state": draw_coarse_state(jax.random.fold_in(splits[3], 71), 0),
        "box_y": draw_box_y(jax.random.fold_in(splits[3], 71), 0),
    }


def starts(*values):
    return tuple((jnp.asarray(v).astype(jnp.int32) for v in values))

def state_parts(state):
    density = state[0]
    inverse = 1.0 / density
    velocity = state[1:4] * inverse
    kinetic = 0.5 * lax.optimization_barrier(jnp.sum(state[1:4] * velocity, axis=0))
    pressure = 0.4 * (state[4] - kinetic)
    sound = jnp.sqrt(1.4 * pressure * inverse)
    return (velocity, pressure, sound)

def speed_max(state):
    velocity, pressure, sound = state_parts(state)
    return jnp.max(lax.optimization_barrier(jnp.sum(jnp.abs(velocity), axis=0)) + 3.0 * sound)

def physical(state, velocity, pressure, along):
    speed = velocity[along]
    parts = [state[0] * speed]
    for comp in range(3):
        term = state[1 + comp] * speed
        if comp == along:
            term = term + pressure
        parts.append(term)
    parts.append((state[4] + pressure) * speed)
    return jnp.stack(parts, axis=0)

def rusanov(left, right, along):
    vel_l, pres_l, snd_l = state_parts(left)
    vel_r, pres_r, snd_r = state_parts(right)
    reach = jnp.maximum(jnp.abs(vel_l[along]) + snd_l, jnp.abs(vel_r[along]) + snd_r)
    return 0.5 * (physical(left, vel_l, pres_l, along) + physical(right, vel_r, pres_r, along)) - 0.5 * reach * (right - left)

def pool_face(face):
    comps, rows_a, rows_b = face.shape
    return face.reshape(comps, rows_a // 2, 2, rows_b // 2, 2).sum(axis=(2, 4)) * 0.25

def box_step(state, padded, anchor_y, step):
    half = BOX // 2
    layers = state.shape[1]
    cols = padded.shape[2]
    anchor_x = 0
    region = lax.dynamic_slice(padded, starts(0, 0, anchor_x, anchor_y - 1), (5, layers // 2, half + 2, half + 2))
    upsampled = jnp.repeat(jnp.repeat(jnp.repeat(region, 2, axis=1), 2, axis=2), 2, axis=3)[:, :, 1:-1, 1:-1]
    ghost = upsampled.at[:, :, 1:-1, 1:-1].set(state)
    zfull = jnp.concatenate([state[:, :1], state, state[:, -1:]], axis=1)
    flux_z = rusanov(zfull[:, :-1], zfull[:, 1:], 0)
    flux_x = rusanov(ghost[:, :, :-1, 1:-1], ghost[:, :, 1:, 1:-1], 1)
    flux_y = rusanov(ghost[:, :, 1:-1, :-1], ghost[:, :, 1:-1, 1:], 2)
    fresh = state - step * (flux_z[:, 1:] - flux_z[:, :-1] + (flux_x[:, :, 1:] - flux_x[:, :, :-1]) + (flux_y[:, :, :, 1:] - flux_y[:, :, :, :-1]))
    share = 0.5 * step
    coarse_xl = rusanov(region[:, :, 0, 1:-1], region[:, :, 1, 1:-1], 1)
    coarse_xh = rusanov(region[:, :, half, 1:-1], region[:, :, half + 1, 1:-1], 1)
    coarse_yl = rusanov(region[:, :, 1:-1, 0], region[:, :, 1:-1, 1], 2)
    coarse_yh = rusanov(region[:, :, 1:-1, half], region[:, :, 1:-1, half + 1], 2)
    corr_xl = share * (coarse_xl - pool_face(flux_x[:, :, 0, :]))
    corr_xh = share * (pool_face(flux_x[:, :, BOX, :]) - coarse_xh)
    corr_yl = share * (coarse_yl - pool_face(flux_y[:, :, :, 0]))
    corr_yh = share * (pool_face(flux_y[:, :, :, BOX]) - coarse_yh)
    delta = jnp.zeros(padded.shape, jnp.float32)
    delta = lax.dynamic_update_slice(delta, corr_xl[:, :, None, :], starts(0, 0, anchor_x, anchor_y))
    delta = lax.dynamic_update_slice(delta, corr_xh[:, :, None, :], starts(0, 0, anchor_x + half + 1, anchor_y))
    delta = lax.dynamic_update_slice(delta, corr_yl[:, :, :, None], starts(0, 0, anchor_x + 1, anchor_y - 1))
    delta = lax.dynamic_update_slice(delta, corr_yh[:, :, :, None], starts(0, 0, anchor_x + 1, anchor_y + half))
    middle = padded[:, :, 1:-1] + delta[:, :, 1:-1]
    average = fresh.reshape(5, layers // 2, 2, half, 2, half, 2).sum(axis=(2, 4, 6)) * 0.125
    return (fresh, middle, delta[:, :, 0], delta[:, :, cols - 1], average)

def reference(fine_state, coarse_state, box_y):
    boxes = fine_state.shape[0]
    half = BOX // 2
    slabs = coarse_state.reshape(5, CZ, boxes, CX, NYC).transpose(2, 0, 1, 3, 4)
    prev_col = jnp.roll(slabs, 1, axis=0)[:, :, :, -1:]
    next_col = jnp.roll(slabs, -1, axis=0)[:, :, :, :1]
    padded = jnp.concatenate([prev_col, slabs, next_col], axis=3)
    fine_boxes = fine_state.reshape(boxes, 5, LAYERS, BOX, BOX)
    fine_top = jnp.max(lax.map(speed_max, fine_boxes))
    smax = jnp.maximum(fine_top, speed_max(coarse_state))
    step = 0.8 / smax

    def one_box(items):
        return box_step(items[0], items[1], items[2], step)
    fresh, middle, left_rims, right_rims, average = lax.map(one_box, (fine_boxes, padded, box_y))
    middle = middle.at[:, :, :, 0].add(jnp.roll(right_rims, 1, axis=0))
    middle = middle.at[:, :, :, -1].add(jnp.roll(left_rims, -1, axis=0))

    def place(items):
        return lax.dynamic_update_slice(items[0], items[1], starts(0, 0, 0, items[2]))
    final = lax.map(place, (middle, average, box_y))
    coarse_next = final.transpose(1, 2, 0, 3, 4).reshape(5, CZ, boxes * CX, NYC)
    return (fresh.reshape(boxes, 5, LAYERS, BOX * BOX), coarse_next)
```

```python
import functools

import jax
import jax.numpy as jnp
from jax import lax
from jax.experimental import pallas as pl
from jax.experimental.pallas import tpu as pltpu
from jax.sharding import PartitionSpec as P

MESH = pl.DeviceIdType.MESH
COMPS = 5


def primitives(state):
    inverse = 1.0 / state[0]
    velocity = [m * inverse for m in state[1:4]]
    kinetic = 0.5 * (
        state[1] * velocity[0] + state[2] * velocity[1] + state[3] * velocity[2]
    )
    pressure = 0.4 * (state[4] - kinetic)
    sound = jnp.sqrt(1.4 * pressure * inverse)
    return velocity, pressure, sound


def speed(state):
    velocity, _, sound = primitives(state)
    return jnp.abs(velocity[0]) + jnp.abs(velocity[1]) + jnp.abs(velocity[2]) + 3.0 * sound


def physical(state, prims, along):
    velocity, pressure, _ = prims
    v = velocity[along]
    parts = [state[1 + along]]
    for comp in range(3):
        term = state[1 + comp] * v
        parts.append(term + pressure if comp == along else term)
    parts.append((state[4] + pressure) * v)
    return parts


def reach(prims, along):
    return jnp.abs(prims[0][along]) + prims[2]


def rusanov(left, right, along):
    pl_, pr = primitives(left), primitives(right)
    a = jnp.maximum(reach(pl_, along), reach(pr, along))
    fl, fr = physical(left, pl_, along), physical(right, pr, along)
    return [0.5 * (fl[c] + fr[c]) - 0.5 * a * (right[c] - left[c]) for c in range(COMPS)]


def top(values):
    return jnp.max(jnp.max(values, axis=0, keepdims=True), axis=1, keepdims=True)


def dot(a, b):
    return jnp.dot(a, b, precision=lax.Precision.HIGHEST, preferred_element_type=jnp.float32)


def advance(
    nb, ns, by_hbm, f4, c3, f2, u_ref, tot, base, gain, info,
    by_ref, c_ref, gl, gu, zl, zh, ch, fh, es, yg, fy,
    msg, slots, anchor, anchors, send_a, recv_a, send_h, recv_h, load, go,
):
    b = lax.axis_index("box")
    s = lax.axis_index("sub")
    rows, lanes = u_ref.shape[1:]
    crows = c_ref.shape[1]
    last_f = f4.shape[1] - 1
    layers = f4.shape[2]
    edge = lanes // 2
    half = edge // 2
    barrier = pltpu.get_barrier_semaphore()
    count = nb * ns
    unroll = count <= 64
    hub = (b == nb - 1) & (s == ns - 1)
    inner_s = (s > 0) & (s < ns - 1)

    def peer(k):
        return (lax.rem(b + lax.rem(k, nb), nb), lax.rem(s + lax.div(k, nb), ns))

    def signal(sem, device):
        pl.semaphore_signal(sem, inc=1, device_id=device, device_id_type=MESH)

    load_u = pltpu.make_async_copy(f2, u_ref, load.at[0])
    load_c = pltpu.make_async_copy(c3, c_ref, load.at[1])
    load_by = pltpu.make_async_copy(by_hbm, by_ref, load.at[2])
    load_c.start()
    load_u.start()
    load_by.start()

    pl.when((s < ns - 2) | ((s == ns - 2) & (b < nb - 1)))(
        lambda: signal(barrier, (nb - 1, ns - 1))
    )
    pl.when(s > 0)(lambda: signal(barrier, (b, s - 1)))
    pl.when(s < ns - 1)(lambda: signal(barrier, (b, s + 1)))

    def hail(k, carry):
        signal(barrier, peer(k))
        return carry

    def release(k, carry):
        signal(go, peer(k))
        return carry

    lax.fori_loop(1, nb, hail, 0, unroll=unroll)

    @pl.when(hub)
    def _():
        pl.semaphore_wait(barrier, count - 1)
        lax.fori_loop(1, count, release, 0, unroll=unroll)

    load_c.wait()
    C = [c_ref[c] for c in range(COMPS)]
    coarse_top = top(speed(C))
    load_u.wait()
    U = [u_ref[c] for c in range(COMPS)]
    fine_top = top(speed(U))
    local = jnp.broadcast_to(jnp.maximum(fine_top, coarse_top), (1, lanes))
    msg[...] = local
    load_by.wait()
    by = by_ref[0]
    anchor[...] = jnp.full((8, lanes), by.astype(jnp.float32))

    for c in range(COMPS):
        zl[c] = u_ref[c, pl.ds(0, crows, stride=2)]
        zh[c] = u_ref[c, pl.ds(1, crows, stride=2)]

    pl.when(inner_s)(lambda: pl.semaphore_wait(barrier, nb + 1))
    pl.when(~inner_s & ~hub)(lambda: pl.semaphore_wait(barrier, nb))

    def remote(src, dst, send, recv, peer):
        return pltpu.make_async_remote_copy(
            src_ref=src, dst_ref=dst, send_sem=send, recv_sem=recv,
            device_id=peer, device_id_type=MESH,
        )

    def tell(k, carry):
        remote(msg, slots.at[pl.ds(k - 1, 1)], send_a, recv_a, peer(k)).start()
        return carry

    lax.fori_loop(1, nb, tell, 0, unroll=unroll)

    def spread_far():
        pl.when(~hub)(lambda: pl.semaphore_wait(go, 1))
        lax.fori_loop(nb, count, tell, 0, unroll=unroll)

    pl.when(2 * s >= ns)(spread_far)

    after, before = peer(1), peer(nb - 1)
    halos = [
        remote(c3.at[:, crows - 1], ch.at[0], send_h.at[0], recv_h.at[0], after),
        remote(c3.at[:, 0], ch.at[1], send_h.at[1], recv_h.at[1], before),
        remote(f4.at[:, last_f], fh.at[0], send_h.at[2], recv_h.at[2], after),
        remote(f4.at[:, 0], fh.at[1], send_h.at[3], recv_h.at[3], before),
        remote(anchor, anchors.at[0], send_h.at[6], recv_h.at[8], after),
        remote(anchor, anchors.at[1], send_h.at[7], recv_h.at[9], before),
    ]
    for copy in halos:
        copy.start()
    up = remote(
        zh, gl, send_h.at[4], recv_h.at[4],
        (b, jnp.minimum(s + 1, ns - 1)),
    )
    down = remote(
        zl, gu, send_h.at[5], recv_h.at[5], (b, jnp.maximum(s - 1, 0))
    )
    own_low = pltpu.make_async_copy(f4.at[:, :, 0], gl, recv_h.at[6])
    own_high = pltpu.make_async_copy(f4.at[:, :, layers - 1], gu, recv_h.at[7])
    pl.when(s < ns - 1)(up.start)
    pl.when(s > 0)(down.start)
    pl.when(s == 0)(own_low.start)
    pl.when(s == ns - 1)(own_high.start)

    sub_i = lax.broadcasted_iota(jnp.int32, (lanes, lanes), 0)
    lane_i = lax.broadcasted_iota(jnp.int32, (lanes, lanes), 1)
    spread_y = (lane_i & (edge - 1)) >> 1
    gather_y = (sub_i & (edge - 1)) >> 1

    def spread(anchor):
        return jnp.where(sub_i == anchor + spread_y, 1.0, 0.0)

    def pool(anchor, weight, keep):
        return jnp.where((lane_i == anchor + gather_y) & keep, weight, 0.0)

    r = lax.broadcasted_iota(jnp.int32, (rows, lanes), 0)
    lane = lax.broadcasted_iota(jnp.int32, (rows, lanes), 1)
    y = lane & (edge - 1)
    odd_l = (r & 1) == 1
    odd_x = lane >= edge
    odd_y = (lane & 1) == 1
    prims = primitives(U)
    clane = lax.broadcasted_iota(jnp.int32, (crows, lanes), 1)
    crow = lax.broadcasted_iota(jnp.int32, (crows, lanes), 0)
    at = clane & (edge - 1)
    for c in range(COMPS):
        low = jnp.sum(jnp.where(clane == by - 1, C[c], 0.0), axis=1, keepdims=True)
        high = jnp.sum(jnp.where(clane == by + half, C[c], 0.0), axis=1, keepdims=True)
        value = jnp.where(at == 0, low, high)
        yg[c, pl.ds(0, crows, stride=2)] = value
        yg[c, pl.ds(1, crows, stride=2)] = value

    def side(total, partner, along, sign):
        pp = primitives(partner)
        a = jnp.maximum(reach(prims, along), reach(pp, along))
        fp = physical(partner, pp, along)
        out = [sign * fp[c] + a * (U[c] - partner[c]) for c in range(COMPS)]
        if total is not None:
            out = [total[c] + out[c] for c in range(COMPS)]
        return out, a, fp

    sz = jnp.where(odd_l, 1.0, -1.0)
    sx = jnp.where(odd_x, 1.0, -1.0)
    sy = jnp.where(odd_y, 1.0, -1.0)
    inner = [
        jnp.where(odd_l, pltpu.roll(u, 1, 0), pltpu.roll(u, rows - 1, 0)) for u in U
    ]
    total, _, _ = side(None, inner, 0, -sz)
    inner = [pltpu.roll(u, edge, 1) for u in U]
    total, _, _ = side(total, inner, 1, -sx)
    low = [pltpu.roll(u, 1, 1) for u in U]
    high = [pltpu.roll(u, lanes - 1, 1) for u in U]
    inner = [jnp.where(odd_y, low[c], high[c]) for c in range(COMPS)]
    total, _, _ = side(total, inner, 2, -sy)
    rim = (y == 0) | (y == edge - 1)
    outer = [
        jnp.where(rim, yg[c], jnp.where(odd_y, high[c], low[c])) for c in range(COMPS)
    ]
    total, a, fp = side(total, outer, 2, sy)
    fu = physical(U, prims, 2)
    for c in range(COMPS):
        fy[c] = 0.5 * (fu[c] + fp[c]) + 0.5 * a * sy * (U[c] - outer[c])
        tot[c] = total[c]
    for c in range(COMPS):
        es[32 + c * crows : 32 + (c + 1) * crows] = (
            u_ref[c, pl.ds(0, crows, stride=2)] + u_ref[c, pl.ds(1, crows, stride=2)]
        )
    pool_own = pool(by, 0.125, sub_i >= 0)
    average = dot(es[32:], pool_own)
    covered = (clane >= by) & (clane < by + half)
    for c in range(COMPS):
        base[c] = jnp.where(covered, average[c * crows : (c + 1) * crows], C[c])

    cy = rusanov(C, [pltpu.roll(v, lanes - 1, 1) for v in C], 2)
    for c in range(COMPS):
        pair = fy[c, pl.ds(0, crows, stride=2)] + fy[c, pl.ds(1, crows, stride=2)]
        ff_lo = 0.25 * jnp.sum(jnp.where(at == 0, pair, 0.0), axis=1, keepdims=True)
        ff_hi = 0.25 * jnp.sum(jnp.where(at == edge - 1, pair, 0.0), axis=1, keepdims=True)
        gain[c] = jnp.where(clane == by - 1, cy[c] - ff_lo, 0.0) + jnp.where(
            clane == by + half, ff_hi - pltpu.roll(cy[c], 1, 1), 0.0
        )

    pl.when((2 * s < ns) & (s > 0))(spread_far)
    for copy in halos:
        copy.wait()
    by_prev = anchors[0, 0:1, :].astype(jnp.int32)
    by_next = anchors[1, 0:1, :].astype(jnp.int32)
    for c in range(COMPS):
        es[c : c + 1] = c_ref[c, 0:1]
        es[8 + c : 9 + c] = c_ref[c, crows - 1 : crows]
        es[16 + c : 17 + c] = ch[0, c : c + 1]
        es[24 + c : 25 + c] = ch[1, c : c + 1]
    ghost_x = dot(es[16:32], spread(by))
    own_up_prev = dot(es[0:8], spread(by_prev))
    own_up_next = dot(es[8:16], spread(by_next))

    total = [tot[c] for c in range(COMPS)]
    outer = []
    for c in range(COMPS):
        v = pltpu.roll(U[c], edge, 1)
        g = jnp.where(odd_x, pltpu.roll(v, rows - 2, 0), pltpu.roll(v, 2, 0))
        g = jnp.where((r < 2) & ~odd_x, ghost_x[c : c + 1], g)
        g = jnp.where((r >= rows - 2) & odd_x, ghost_x[8 + c : 9 + c], g)
        outer.append(g)
    total, _, _ = side(total, outer, 1, sx)

    split = lambda v, k: [v[k + c : k + c + 1] for c in range(COMPS)]
    own_lo, own_hi, prev, nxt = (split(es[0:32], k) for k in (0, 8, 16, 24))
    fine_prev = [fh[0, c] for c in range(COMPS)]
    fine_next = [fh[1, c] for c in range(COMPS)]
    wide = lambda v: [jnp.broadcast_to(w, fine_prev[0].shape) for w in v]
    ff_prev = rusanov(fine_prev, wide(split(own_up_prev, 0)), 1)
    ff_next = rusanov(wide(split(own_up_next, 0)), fine_next, 1)
    fc_prev = rusanov(prev, own_lo, 1)
    fc_next = rusanov(own_hi, nxt, 1)
    for c in range(COMPS):
        es[c : c + 1] = jnp.sum(ff_prev[c], axis=0, keepdims=True)
        es[8 + c : 9 + c] = jnp.sum(ff_next[c], axis=0, keepdims=True)
    upper_half = sub_i >= edge
    pooled_prev = dot(es[0:8], pool(by_prev, 0.25, upper_half))
    pooled_next = dot(es[8:16], pool(by_next, 0.25, ~upper_half))
    one = lax.broadcasted_iota(jnp.int32, (1, lanes), 1)
    in_prev = (one >= by_prev) & (one < by_prev + half)
    in_next = (one >= by_next) & (one < by_next + half)

    pl.when(s > 0)(up.wait_recv)
    pl.when(s < ns - 1)(down.wait_recv)
    pl.when(s == 0)(own_low.wait)
    pl.when(s == ns - 1)(own_high.wait)
    for c in range(COMPS):
        yg[c, pl.ds(0, crows, stride=2)] = gl[c]
        yg[c, pl.ds(1, crows, stride=2)] = gu[c]
    total, _, _ = side(total, [yg[c] for c in range(COMPS)], 0, sz)
    for c in range(COMPS):
        tot[c] = total[c]

    for c in range(COMPS):
        es[32 + c * crows : 32 + (c + 1) * crows] = (
            tot[c, pl.ds(0, crows, stride=2)] + tot[c, pl.ds(1, crows, stride=2)]
        )
    average = dot(es[32:], pool_own)
    for c in range(COMPS):
        low = jnp.where(in_prev, pooled_prev[c : c + 1] - fc_prev[c], 0.0)
        high = jnp.where(in_next, fc_next[c] - pooled_next[c : c + 1], 0.0)
        out = gain[c] + jnp.where(crow == 0, low, 0.0)
        out = out + jnp.where(crow == crows - 1, high, 0.0)
        gain[c] = jnp.where(covered, -average[c * crows : (c + 1) * crows], out)

    pl.when((2 * s < ns) & (s == 0))(spread_far)
    told = slots.at[pl.ds(0, count - 1)]
    pltpu.make_async_copy(told, told, recv_a).wait()
    srow = lax.broadcasted_iota(jnp.int32, slots.shape, 0)
    merged = jnp.max(jnp.where(srow < count - 1, slots[...], local), axis=0, keepdims=True)
    info[...] = jnp.broadcast_to(merged, info.shape)
    pl.when(s < ns - 1)(up.wait_send)
    pl.when(s > 0)(down.wait_send)
    pltpu.make_async_copy(told, told, send_a).wait()


def finish(u_ref, tot, base, gain, info, fo, co):
    hdt = 0.5 * (0.8 / info[0:1, :])
    for c in range(COMPS):
        fo[c] = u_ref[c] - hdt * tot[c]
        co[c] = base[c] + hdt * gain[c]


def shards(nb, ns, fine_state, coarse_state, box_y):
    layers, cells = fine_state.shape[2:]
    lanes = coarse_state.shape[3]
    crows = coarse_state.shape[2]
    blocks = cells // lanes
    rows = blocks * layers
    f4 = fine_state[0].reshape(COMPS, layers, blocks, lanes).transpose(0, 2, 1, 3)
    f2 = f4.reshape(COMPS, rows, lanes)
    c3 = coarse_state.reshape(COMPS, crows, lanes)
    f32 = lambda *shape: jax.ShapeDtypeStruct(shape, jnp.float32)
    buf = lambda *shape: pltpu.VMEM(shape, jnp.float32)
    vmem = pl.BlockSpec(memory_space=pltpu.VMEM)
    hbm = pl.BlockSpec(memory_space=pltpu.HBM)
    fine = (COMPS, rows, lanes)
    coarse = (COMPS, crows, lanes)
    dma = pltpu.SemaphoreType.DMA
    u, tot, base, gain, info = pl.pallas_call(
        functools.partial(advance, nb, ns),
        out_shape=(buf(*fine), buf(*fine), buf(*coarse), buf(*coarse), buf(8, lanes)),
        in_specs=[hbm, hbm, hbm, hbm],
        out_specs=(vmem,) * 5,
        scratch_shapes=[
            pltpu.SMEM((1,), jnp.int32), buf(*coarse), buf(*coarse), buf(*coarse),
            buf(*coarse), buf(*coarse),
            buf(2, COMPS, lanes), buf(2, COMPS, layers, lanes),
            buf(32 + COMPS * crows, lanes), buf(*fine), buf(*fine),
            buf(1, lanes), buf(nb * ns, lanes), buf(8, lanes), buf(2, 8, lanes),
            dma, dma, dma((8,)), dma((10,)), dma((3,)), pltpu.SemaphoreType.REGULAR,
        ],
        compiler_params=pltpu.CompilerParams(collective_id=0, has_side_effects=True),
        name="advance",
    )(box_y, f4, c3, f2)
    fo, co = pl.pallas_call(
        finish,
        out_shape=(f32(*fine), f32(*coarse)),
        in_specs=[vmem] * 5,
        out_specs=(vmem, vmem),
        name="finish",
    )(*(pltpu.with_memory_space_constraint(v, pltpu.VMEM) for v in (u, tot, base, gain, info)))
    fresh = fo.reshape(COMPS, blocks, layers, lanes).transpose(0, 2, 1, 3)
    return fresh.reshape(1, COMPS, layers, cells), co.reshape(coarse_state.shape)


def solution(mesh):
    placed = (P("box", None, "sub", None), P(None, "sub", "box", None), P("box"))
    return jax.shard_map(
        functools.partial(shards, mesh.shape["box"], mesh.shape["sub"]),
        mesh=mesh,
        in_specs=placed,
        out_specs=(P("box", None, "sub", None), P(None, "sub", "box", None)),
        check_vma=False,
    )
```

```python
import functools

import jax
import jax.numpy as jnp
from jax import lax
from jax.experimental import pallas as pl
from jax.experimental.pallas import tpu as pltpu
from jax.sharding import PartitionSpec as P

MESH = pl.DeviceIdType.MESH
COMPS = 5


def primitives(state):
    inverse = 1.0 / state[0]
    velocity = [m * inverse for m in state[1:4]]
    kinetic = 0.5 * (
        state[1] * velocity[0] + state[2] * velocity[1] + state[3] * velocity[2]
    )
    pressure = 0.4 * (state[4] - kinetic)
    sound = jnp.sqrt(1.4 * pressure * inverse)
    return velocity, pressure, sound


def speed(state):
    velocity, _, sound = primitives(state)
    return jnp.abs(velocity[0]) + jnp.abs(velocity[1]) + jnp.abs(velocity[2]) + 3.0 * sound


def physical(state, prims, along):
    velocity, pressure, _ = prims
    v = velocity[along]
    parts = [state[1 + along]]
    for comp in range(3):
        term = state[1 + comp] * v
        parts.append(term + pressure if comp == along else term)
    parts.append((state[4] + pressure) * v)
    return parts


def reach(prims, along):
    return jnp.abs(prims[0][along]) + prims[2]


def rusanov(left, right, along):
    pl_, pr = primitives(left), primitives(right)
    a = jnp.maximum(reach(pl_, along), reach(pr, along))
    fl, fr = physical(left, pl_, along), physical(right, pr, along)
    return [0.5 * (fl[c] + fr[c]) - 0.5 * a * (right[c] - left[c]) for c in range(COMPS)]


def top(values):
    return jnp.max(jnp.max(values, axis=0, keepdims=True), axis=1, keepdims=True)


def dot(a, b):
    return jnp.dot(a, b, precision=lax.Precision.HIGHEST, preferred_element_type=jnp.float32)


def advance(
    nb, ns, by_hbm, f4, c3, f2, u_ref, tot, base, gain, info,
    by_ref, c_ref, gl, gu, zl, zh, ch, fh, es, yg, fy,
    msg, slots, anchor, anchors, send_a, recv_a, send_h, recv_h, load, go,
):
    b = lax.axis_index("box")
    s = lax.axis_index("sub")
    rows, lanes = u_ref.shape[1:]
    crows = c_ref.shape[1]
    last_f = f4.shape[1] - 1
    layers = f4.shape[2]
    edge = lanes // 2
    half = edge // 2
    barrier = pltpu.get_barrier_semaphore()
    count = nb * ns
    unroll = count <= 64
    last_s = s == ns - 1

    def peer(k):
        return (lax.rem(b + lax.rem(k, nb), nb), lax.rem(s + lax.div(k, nb), ns))

    above = nb * (ns - s)

    def signal(sem, device):
        pl.semaphore_signal(sem, inc=1, device_id=device, device_id_type=MESH)

    load_u = pltpu.make_async_copy(f2, u_ref, load.at[0])
    load_c = pltpu.make_async_copy(c3, c_ref, load.at[1])
    load_by = pltpu.make_async_copy(by_hbm, by_ref, load.at[2])
    load_c.start()
    load_u.start()
    load_by.start()

    def hail(k, carry):
        signal(barrier, peer(k))
        return carry

    pl.when(s > 0)(lambda: signal(barrier, (b, s - 1)))
    lax.fori_loop(1, above, hail, 0)

    load_c.wait()
    C = [c_ref[c] for c in range(COMPS)]
    coarse_top = top(speed(C))
    load_u.wait()
    U = [u_ref[c] for c in range(COMPS)]
    fine_top = top(speed(U))
    local = jnp.broadcast_to(jnp.maximum(fine_top, coarse_top), (1, lanes))
    msg[...] = local
    load_by.wait()
    by = by_ref[0]
    anchor[...] = jnp.full((8, lanes), by.astype(jnp.float32))

    for c in range(COMPS):
        zl[c] = u_ref[c, pl.ds(0, crows, stride=2)]
        zh[c] = u_ref[c, pl.ds(1, crows, stride=2)]

    heard = nb * (s + 1) - 1
    pl.when(last_s)(lambda: pl.semaphore_wait(barrier, heard))
    pl.when(~last_s)(lambda: pl.semaphore_wait(barrier, heard + 1))

    @pl.when(last_s)
    def _():
        for j in range(ns - 1):
            signal(go, (b, j))

    def remote(src, dst, send, recv, peer):
        return pltpu.make_async_remote_copy(
            src_ref=src, dst_ref=dst, send_sem=send, recv_sem=recv,
            device_id=peer, device_id_type=MESH,
        )

    def tell(k, carry):
        remote(msg, slots.at[pl.ds(k - 1, 1)], send_a, recv_a, peer(k)).start()
        return carry

    lax.fori_loop(above, count, tell, 0)
    lax.fori_loop(1, nb, tell, 0, unroll=unroll)

    def spread_up():
        pl.semaphore_wait(go, 1)
        lax.fori_loop(nb, above, tell, 0)

    after, before = peer(1), peer(nb - 1)
    halos = [
        remote(c3.at[:, crows - 1], ch.at[0], send_h.at[0], recv_h.at[0], after),
        remote(c3.at[:, 0], ch.at[1], send_h.at[1], recv_h.at[1], before),
        remote(f4.at[:, last_f], fh.at[0], send_h.at[2], recv_h.at[2], after),
        remote(f4.at[:, 0], fh.at[1], send_h.at[3], recv_h.at[3], before),
        remote(anchor, anchors.at[0], send_h.at[6], recv_h.at[8], after),
        remote(anchor, anchors.at[1], send_h.at[7], recv_h.at[9], before),
    ]
    for copy in halos:
        copy.start()
    up = remote(
        zh, gl, send_h.at[4], recv_h.at[4],
        (b, jnp.minimum(s + 1, ns - 1)),
    )
    down = remote(
        zl, gu, send_h.at[5], recv_h.at[5], (b, jnp.maximum(s - 1, 0))
    )
    own_low = pltpu.make_async_copy(f4.at[:, :, 0], gl, recv_h.at[6])
    own_high = pltpu.make_async_copy(f4.at[:, :, layers - 1], gu, recv_h.at[7])
    pl.when(s < ns - 1)(up.start)
    pl.when(s > 0)(down.start)
    pl.when(s == 0)(own_low.start)
    pl.when(s == ns - 1)(own_high.start)

    sub_i = lax.broadcasted_iota(jnp.int32, (lanes, lanes), 0)
    lane_i = lax.broadcasted_iota(jnp.int32, (lanes, lanes), 1)
    spread_y = (lane_i & (edge - 1)) >> 1
    gather_y = (sub_i & (edge - 1)) >> 1

    def spread(anchor):
        return jnp.where(sub_i == anchor + spread_y, 1.0, 0.0)

    def pool(anchor, weight, keep):
        return jnp.where((lane_i == anchor + gather_y) & keep, weight, 0.0)

    r = lax.broadcasted_iota(jnp.int32, (rows, lanes), 0)
    lane = lax.broadcasted_iota(jnp.int32, (rows, lanes), 1)
    y = lane & (edge - 1)
    odd_l = (r & 1) == 1
    odd_x = lane >= edge
    odd_y = (lane & 1) == 1
    prims = primitives(U)
    clane = lax.broadcasted_iota(jnp.int32, (crows, lanes), 1)
    crow = lax.broadcasted_iota(jnp.int32, (crows, lanes), 0)
    at = clane & (edge - 1)
    for c in range(COMPS):
        low = jnp.sum(jnp.where(clane == by - 1, C[c], 0.0), axis=1, keepdims=True)
        high = jnp.sum(jnp.where(clane == by + half, C[c], 0.0), axis=1, keepdims=True)
        value = jnp.where(at == 0, low, high)
        yg[c, pl.ds(0, crows, stride=2)] = value
        yg[c, pl.ds(1, crows, stride=2)] = value

    def side(total, partner, along, sign):
        pp = primitives(partner)
        a = jnp.maximum(reach(prims, along), reach(pp, along))
        fp = physical(partner, pp, along)
        out = [sign * fp[c] + a * (U[c] - partner[c]) for c in range(COMPS)]
        if total is not None:
            out = [total[c] + out[c] for c in range(COMPS)]
        return out, a, fp

    sz = jnp.where(odd_l, 1.0, -1.0)
    sx = jnp.where(odd_x, 1.0, -1.0)
    sy = jnp.where(odd_y, 1.0, -1.0)
    inner = [
        jnp.where(odd_l, pltpu.roll(u, 1, 0), pltpu.roll(u, rows - 1, 0)) for u in U
    ]
    total, _, _ = side(None, inner, 0, -sz)
    inner = [pltpu.roll(u, edge, 1) for u in U]
    total, _, _ = side(total, inner, 1, -sx)
    low = [pltpu.roll(u, 1, 1) for u in U]
    high = [pltpu.roll(u, lanes - 1, 1) for u in U]
    inner = [jnp.where(odd_y, low[c], high[c]) for c in range(COMPS)]
    total, _, _ = side(total, inner, 2, -sy)
    rim = (y == 0) | (y == edge - 1)
    outer = [
        jnp.where(rim, yg[c], jnp.where(odd_y, high[c], low[c])) for c in range(COMPS)
    ]
    total, a, fp = side(total, outer, 2, sy)
    fu = physical(U, prims, 2)
    for c in range(COMPS):
        fy[c] = 0.5 * (fu[c] + fp[c]) + 0.5 * a * sy * (U[c] - outer[c])
        tot[c] = total[c]
    for c in range(COMPS):
        es[32 + c * crows : 32 + (c + 1) * crows] = (
            u_ref[c, pl.ds(0, crows, stride=2)] + u_ref[c, pl.ds(1, crows, stride=2)]
        )
    pool_own = pool(by, 0.125, sub_i >= 0)
    average = dot(es[32:], pool_own)
    covered = (clane >= by) & (clane < by + half)
    for c in range(COMPS):
        base[c] = jnp.where(covered, average[c * crows : (c + 1) * crows], C[c])

    cy = rusanov(C, [pltpu.roll(v, lanes - 1, 1) for v in C], 2)
    for c in range(COMPS):
        pair = fy[c, pl.ds(0, crows, stride=2)] + fy[c, pl.ds(1, crows, stride=2)]
        ff_lo = 0.25 * jnp.sum(jnp.where(at == 0, pair, 0.0), axis=1, keepdims=True)
        ff_hi = 0.25 * jnp.sum(jnp.where(at == edge - 1, pair, 0.0), axis=1, keepdims=True)
        gain[c] = jnp.where(clane == by - 1, cy[c] - ff_lo, 0.0) + jnp.where(
            clane == by + half, ff_hi - pltpu.roll(cy[c], 1, 1), 0.0
        )

    pl.when(~last_s)(spread_up)
    for copy in halos:
        copy.wait()
    by_prev = anchors[0, 0:1, :].astype(jnp.int32)
    by_next = anchors[1, 0:1, :].astype(jnp.int32)
    for c in range(COMPS):
        es[c : c + 1] = c_ref[c, 0:1]
        es[8 + c : 9 + c] = c_ref[c, crows - 1 : crows]
        es[16 + c : 17 + c] = ch[0, c : c + 1]
        es[24 + c : 25 + c] = ch[1, c : c + 1]
    ghost_x = dot(es[16:32], spread(by))
    own_up_prev = dot(es[0:8], spread(by_prev))
    own_up_next = dot(es[8:16], spread(by_next))

    total = [tot[c] for c in range(COMPS)]
    outer = []
    for c in range(COMPS):
        v = pltpu.roll(U[c], edge, 1)
        g = jnp.where(odd_x, pltpu.roll(v, rows - 2, 0), pltpu.roll(v, 2, 0))
        g = jnp.where((r < 2) & ~odd_x, ghost_x[c : c + 1], g)
        g = jnp.where((r >= rows - 2) & odd_x, ghost_x[8 + c : 9 + c], g)
        outer.append(g)
    total, _, _ = side(total, outer, 1, sx)

    split = lambda v, k: [v[k + c : k + c + 1] for c in range(COMPS)]
    own_lo, own_hi, prev, nxt = (split(es[0:32], k) for k in (0, 8, 16, 24))
    fine_prev = [fh[0, c] for c in range(COMPS)]
    fine_next = [fh[1, c] for c in range(COMPS)]
    wide = lambda v: [jnp.broadcast_to(w, fine_prev[0].shape) for w in v]
    ff_prev = rusanov(fine_prev, wide(split(own_up_prev, 0)), 1)
    ff_next = rusanov(wide(split(own_up_next, 0)), fine_next, 1)
    fc_prev = rusanov(prev, own_lo, 1)
    fc_next = rusanov(own_hi, nxt, 1)
    for c in range(COMPS):
        es[c : c + 1] = jnp.sum(ff_prev[c], axis=0, keepdims=True)
        es[8 + c : 9 + c] = jnp.sum(ff_next[c], axis=0, keepdims=True)
    upper_half = sub_i >= edge
    pooled_prev = dot(es[0:8], pool(by_prev, 0.25, upper_half))
    pooled_next = dot(es[8:16], pool(by_next, 0.25, ~upper_half))
    one = lax.broadcasted_iota(jnp.int32, (1, lanes), 1)
    in_prev = (one >= by_prev) & (one < by_prev + half)
    in_next = (one >= by_next) & (one < by_next + half)

    pl.when(s > 0)(up.wait_recv)
    pl.when(s < ns - 1)(down.wait_recv)
    pl.when(s == 0)(own_low.wait)
    pl.when(s == ns - 1)(own_high.wait)
    for c in range(COMPS):
        yg[c, pl.ds(0, crows, stride=2)] = gl[c]
        yg[c, pl.ds(1, crows, stride=2)] = gu[c]
    total, _, _ = side(total, [yg[c] for c in range(COMPS)], 0, sz)
    for c in range(COMPS):
        tot[c] = total[c]

    for c in range(COMPS):
        es[32 + c * crows : 32 + (c + 1) * crows] = (
            tot[c, pl.ds(0, crows, stride=2)] + tot[c, pl.ds(1, crows, stride=2)]
        )
    average = dot(es[32:], pool_own)
    for c in range(COMPS):
        low = jnp.where(in_prev, pooled_prev[c : c + 1] - fc_prev[c], 0.0)
        high = jnp.where(in_next, fc_next[c] - pooled_next[c : c + 1], 0.0)
        out = gain[c] + jnp.where(crow == 0, low, 0.0)
        out = out + jnp.where(crow == crows - 1, high, 0.0)
        gain[c] = jnp.where(covered, -average[c * crows : (c + 1) * crows], out)

    told = slots.at[pl.ds(0, count - 1)]
    pltpu.make_async_copy(told, told, recv_a).wait()
    srow = lax.broadcasted_iota(jnp.int32, slots.shape, 0)
    merged = jnp.max(jnp.where(srow < count - 1, slots[...], local), axis=0, keepdims=True)
    info[...] = jnp.broadcast_to(merged, info.shape)
    pl.when(s < ns - 1)(up.wait_send)
    pl.when(s > 0)(down.wait_send)
    pltpu.make_async_copy(told, told, send_a).wait()


def finish(u_ref, tot, base, gain, info, fo, co):
    hdt = 0.5 * (0.8 / info[0:1, :])
    for c in range(COMPS):
        fo[c] = u_ref[c] - hdt * tot[c]
        co[c] = base[c] + hdt * gain[c]


def shards(nb, ns, fine_state, coarse_state, box_y):
    layers, cells = fine_state.shape[2:]
    lanes = coarse_state.shape[3]
    crows = coarse_state.shape[2]
    blocks = cells // lanes
    rows = blocks * layers
    f4 = fine_state[0].reshape(COMPS, layers, blocks, lanes).transpose(0, 2, 1, 3)
    f2 = f4.reshape(COMPS, rows, lanes)
    c3 = coarse_state.reshape(COMPS, crows, lanes)
    f32 = lambda *shape: jax.ShapeDtypeStruct(shape, jnp.float32)
    buf = lambda *shape: pltpu.VMEM(shape, jnp.float32)
    vmem = pl.BlockSpec(memory_space=pltpu.VMEM)
    hbm = pl.BlockSpec(memory_space=pltpu.HBM)
    fine = (COMPS, rows, lanes)
    coarse = (COMPS, crows, lanes)
    dma = pltpu.SemaphoreType.DMA
    u, tot, base, gain, info = pl.pallas_call(
        functools.partial(advance, nb, ns),
        out_shape=(buf(*fine), buf(*fine), buf(*coarse), buf(*coarse), buf(8, lanes)),
        in_specs=[hbm, hbm, hbm, hbm],
        out_specs=(vmem,) * 5,
        scratch_shapes=[
            pltpu.SMEM((1,), jnp.int32), buf(*coarse), buf(*coarse), buf(*coarse),
            buf(*coarse), buf(*coarse),
            buf(2, COMPS, lanes), buf(2, COMPS, layers, lanes),
            buf(32 + COMPS * crows, lanes), buf(*fine), buf(*fine),
            buf(1, lanes), buf(nb * ns, lanes), buf(8, lanes), buf(2, 8, lanes),
            dma, dma, dma((8,)), dma((10,)), dma((3,)), pltpu.SemaphoreType.REGULAR,
        ],
        compiler_params=pltpu.CompilerParams(collective_id=0, has_side_effects=True),
        name="advance",
    )(box_y, f4, c3, f2)
    fo, co = pl.pallas_call(
        finish,
        out_shape=(f32(*fine), f32(*coarse)),
        in_specs=[vmem] * 5,
        out_specs=(vmem, vmem),
        name="finish",
    )(*(pltpu.with_memory_space_constraint(v, pltpu.VMEM) for v in (u, tot, base, gain, info)))
    fresh = fo.reshape(COMPS, blocks, layers, lanes).transpose(0, 2, 1, 3)
    return fresh.reshape(1, COMPS, layers, cells), co.reshape(coarse_state.shape)


def solution(mesh):
    placed = (P("box", None, "sub", None), P(None, "sub", "box", None), P("box"))
    return jax.shard_map(
        functools.partial(shards, mesh.shape["box"], mesh.shape["sub"]),
        mesh=mesh,
        in_specs=placed,
        out_specs=(P("box", None, "sub", None), P(None, "sub", "box", None)),
        check_vma=False,
    )
```

```python
import functools

import jax
import jax.numpy as jnp
from jax import lax
from jax.experimental import pallas as pl
from jax.experimental.pallas import tpu as pltpu
from jax.sharding import PartitionSpec as P

MESH = pl.DeviceIdType.MESH
COMPS = 5


def primitives(state):
    inverse = 1.0 / state[0]
    velocity = [m * inverse for m in state[1:4]]
    kinetic = 0.5 * (
        state[1] * velocity[0] + state[2] * velocity[1] + state[3] * velocity[2]
    )
    pressure = 0.4 * (state[4] - kinetic)
    sound = jnp.sqrt(1.4 * pressure * inverse)
    return velocity, pressure, sound


def speed(state):
    velocity, _, sound = primitives(state)
    return jnp.abs(velocity[0]) + jnp.abs(velocity[1]) + jnp.abs(velocity[2]) + 3.0 * sound


def physical(state, prims, along):
    velocity, pressure, _ = prims
    v = velocity[along]
    parts = [state[1 + along]]
    for comp in range(3):
        term = state[1 + comp] * v
        parts.append(term + pressure if comp == along else term)
    parts.append((state[4] + pressure) * v)
    return parts


def reach(prims, along):
    return jnp.abs(prims[0][along]) + prims[2]


def rusanov(left, right, along):
    pl_, pr = primitives(left), primitives(right)
    a = jnp.maximum(reach(pl_, along), reach(pr, along))
    fl, fr = physical(left, pl_, along), physical(right, pr, along)
    return [0.5 * (fl[c] + fr[c]) - 0.5 * a * (right[c] - left[c]) for c in range(COMPS)]


def top(values):
    return jnp.max(jnp.max(values, axis=0, keepdims=True), axis=1, keepdims=True)


def dot(a, b):
    return jnp.dot(a, b, precision=lax.Precision.HIGHEST, preferred_element_type=jnp.float32)


def advance(
    nb, ns, by_ref, f4, c3, f2, u_ref, tot, base, gain, info,
    c_ref, gl, gu, zl, zh, ch, fh, es, yg, fy,
    msg, slots, anchor, anchors, send_a, recv_a, send_h, recv_h, load, go,
):
    b = lax.axis_index("box")
    s = lax.axis_index("sub")
    rows, lanes = u_ref.shape[1:]
    crows = c_ref.shape[1]
    last_f = f4.shape[1] - 1
    layers = f4.shape[2]
    edge = lanes // 2
    half = edge // 2
    barrier = pltpu.get_barrier_semaphore()
    count = nb * ns
    unroll = count <= 64
    last_s = s == ns - 1

    def peer(k):
        return (lax.rem(b + lax.rem(k, nb), nb), lax.rem(s + lax.div(k, nb), ns))

    above = nb * (ns - s)

    def signal(sem, device):
        pl.semaphore_signal(sem, inc=1, device_id=device, device_id_type=MESH)

    load_u = pltpu.make_async_copy(f2, u_ref, load.at[0])
    load_c = pltpu.make_async_copy(c3, c_ref, load.at[1])
    load_c.start()
    load_u.start()

    def hail(k, carry):
        signal(barrier, peer(k))
        return carry

    pl.when(s > 0)(lambda: signal(barrier, (b, s - 1)))
    lax.fori_loop(1, above, hail, 0)

    load_c.wait()
    C = [c_ref[c] for c in range(COMPS)]
    coarse_top = speed(C)
    load_u.wait()
    U = [u_ref[c] for c in range(COMPS)]
    fine_top = speed(U)
    for k in range(0, rows, crows):
        coarse_top = jnp.maximum(coarse_top, fine_top[k : k + crows])
    local = jnp.broadcast_to(top(coarse_top), (1, lanes))
    msg[...] = local
    by = by_ref[0]
    anchor[...] = jnp.full((8, lanes), by.astype(jnp.float32))

    for c in range(COMPS):
        zl[c] = u_ref[c, pl.ds(0, crows, stride=2)]
        zh[c] = u_ref[c, pl.ds(1, crows, stride=2)]

    heard = nb * (s + 1) - 1
    pl.when(last_s)(lambda: pl.semaphore_wait(barrier, heard))
    pl.when(~last_s)(lambda: pl.semaphore_wait(barrier, heard + 1))

    @pl.when(last_s)
    def _():
        for j in range(ns - 1):
            signal(go, (b, j))

    def remote(src, dst, send, recv, peer):
        return pltpu.make_async_remote_copy(
            src_ref=src, dst_ref=dst, send_sem=send, recv_sem=recv,
            device_id=peer, device_id_type=MESH,
        )

    def tell(k, carry):
        remote(msg, slots.at[pl.ds(k - 1, 1)], send_a, recv_a, peer(k)).start()
        return carry

    lax.fori_loop(above, count, tell, 0)
    lax.fori_loop(1, nb, tell, 0, unroll=unroll)

    def spread_up():
        pl.semaphore_wait(go, 1)
        lax.fori_loop(nb, above, tell, 0)

    after, before = peer(1), peer(nb - 1)
    halos = [
        remote(c3.at[:, crows - 1], ch.at[0], send_h.at[0], recv_h.at[0], after),
        remote(c3.at[:, 0], ch.at[1], send_h.at[1], recv_h.at[1], before),
        remote(f4.at[:, last_f], fh.at[0], send_h.at[2], recv_h.at[2], after),
        remote(f4.at[:, 0], fh.at[1], send_h.at[3], recv_h.at[3], before),
        remote(anchor, anchors.at[0], send_h.at[6], recv_h.at[8], after),
        remote(anchor, anchors.at[1], send_h.at[7], recv_h.at[9], before),
    ]
    for copy in halos:
        copy.start()
    up = remote(
        zh, gl, send_h.at[4], recv_h.at[4],
        (b, jnp.minimum(s + 1, ns - 1)),
    )
    down = remote(
        zl, gu, send_h.at[5], recv_h.at[5], (b, jnp.maximum(s - 1, 0))
    )
    own_low = pltpu.make_async_copy(f4.at[:, :, 0], gl, recv_h.at[6])
    own_high = pltpu.make_async_copy(f4.at[:, :, layers - 1], gu, recv_h.at[7])
    pl.when(s < ns - 1)(up.start)
    pl.when(s > 0)(down.start)
    pl.when(s == 0)(own_low.start)
    pl.when(s == ns - 1)(own_high.start)

    sub_i = lax.broadcasted_iota(jnp.int32, (lanes, lanes), 0)
    lane_i = lax.broadcasted_iota(jnp.int32, (lanes, lanes), 1)
    spread_y = (lane_i & (edge - 1)) >> 1
    gather_y = (sub_i & (edge - 1)) >> 1

    def spread(anchor):
        return jnp.where(sub_i == anchor + spread_y, 1.0, 0.0)

    def pool(anchor, weight, keep):
        return jnp.where((lane_i == anchor + gather_y) & keep, weight, 0.0)

    r = lax.broadcasted_iota(jnp.int32, (rows, lanes), 0)
    lane = lax.broadcasted_iota(jnp.int32, (rows, lanes), 1)
    y = lane & (edge - 1)
    odd_l = (r & 1) == 1
    odd_x = lane >= edge
    odd_y = (lane & 1) == 1
    prims = primitives(U)
    clane = lax.broadcasted_iota(jnp.int32, (crows, lanes), 1)
    crow = lax.broadcasted_iota(jnp.int32, (crows, lanes), 0)
    at = clane & (edge - 1)
    for c in range(COMPS):
        low = jnp.sum(jnp.where(clane == by - 1, C[c], 0.0), axis=1, keepdims=True)
        high = jnp.sum(jnp.where(clane == by + half, C[c], 0.0), axis=1, keepdims=True)
        value = jnp.where(at == 0, low, high)
        yg[c, pl.ds(0, crows, stride=2)] = value
        yg[c, pl.ds(1, crows, stride=2)] = value

    def side(total, partner, along, sign):
        pp = primitives(partner)
        a = jnp.maximum(reach(prims, along), reach(pp, along))
        fp = physical(partner, pp, along)
        out = [sign * fp[c] + a * (U[c] - partner[c]) for c in range(COMPS)]
        if total is not None:
            out = [total[c] + out[c] for c in range(COMPS)]
        return out, a, fp

    sz = jnp.where(odd_l, 1.0, -1.0)
    sx = jnp.where(odd_x, 1.0, -1.0)
    sy = jnp.where(odd_y, 1.0, -1.0)
    inner = [
        jnp.where(odd_l, pltpu.roll(u, 1, 0), pltpu.roll(u, rows - 1, 0)) for u in U
    ]
    total, _, _ = side(None, inner, 0, -sz)
    inner = [pltpu.roll(u, edge, 1) for u in U]
    total, _, _ = side(total, inner, 1, -sx)
    low = [pltpu.roll(u, 1, 1) for u in U]
    high = [pltpu.roll(u, lanes - 1, 1) for u in U]
    inner = [jnp.where(odd_y, low[c], high[c]) for c in range(COMPS)]
    total, _, _ = side(total, inner, 2, -sy)
    rim = (y == 0) | (y == edge - 1)
    outer = [
        jnp.where(rim, yg[c], jnp.where(odd_y, high[c], low[c])) for c in range(COMPS)
    ]
    total, a, fp = side(total, outer, 2, sy)
    fu = physical(U, prims, 2)
    for c in range(COMPS):
        fy[c] = 0.5 * (fu[c] + fp[c]) + 0.5 * a * sy * (U[c] - outer[c])
        tot[c] = total[c]
    for c in range(COMPS):
        es[32 + c * crows : 32 + (c + 1) * crows] = (
            u_ref[c, pl.ds(0, crows, stride=2)] + u_ref[c, pl.ds(1, crows, stride=2)]
        )
    pool_own = pool(by, 0.125, sub_i >= 0)
    average = dot(es[32:], pool_own)
    covered = (clane >= by) & (clane < by + half)
    for c in range(COMPS):
        base[c] = jnp.where(covered, average[c * crows : (c + 1) * crows], C[c])

    cy = rusanov(C, [pltpu.roll(v, lanes - 1, 1) for v in C], 2)
    for c in range(COMPS):
        pair = fy[c, pl.ds(0, crows, stride=2)] + fy[c, pl.ds(1, crows, stride=2)]
        ff_lo = 0.25 * jnp.sum(jnp.where(at == 0, pair, 0.0), axis=1, keepdims=True)
        ff_hi = 0.25 * jnp.sum(jnp.where(at == edge - 1, pair, 0.0), axis=1, keepdims=True)
        gain[c] = jnp.where(clane == by - 1, cy[c] - ff_lo, 0.0) + jnp.where(
            clane == by + half, ff_hi - pltpu.roll(cy[c], 1, 1), 0.0
        )

    pl.when(~last_s)(spread_up)
    for copy in halos:
        copy.wait()
    by_prev = anchors[0, 0:1, :].astype(jnp.int32)
    by_next = anchors[1, 0:1, :].astype(jnp.int32)
    for c in range(COMPS):
        es[c : c + 1] = c_ref[c, 0:1]
        es[8 + c : 9 + c] = c_ref[c, crows - 1 : crows]
        es[16 + c : 17 + c] = ch[0, c : c + 1]
        es[24 + c : 25 + c] = ch[1, c : c + 1]
    ghost_x = dot(es[16:32], spread(by))
    own_up_prev = dot(es[0:8], spread(by_prev))
    own_up_next = dot(es[8:16], spread(by_next))

    total = [tot[c] for c in range(COMPS)]
    outer = []
    for c in range(COMPS):
        v = pltpu.roll(U[c], edge, 1)
        g = jnp.where(odd_x, pltpu.roll(v, rows - 2, 0), pltpu.roll(v, 2, 0))
        g = jnp.where((r < 2) & ~odd_x, ghost_x[c : c + 1], g)
        g = jnp.where((r >= rows - 2) & odd_x, ghost_x[8 + c : 9 + c], g)
        outer.append(g)
    total, _, _ = side(total, outer, 1, sx)

    split = lambda v, k: [v[k + c : k + c + 1] for c in range(COMPS)]
    own_lo, own_hi, prev, nxt = (split(es[0:32], k) for k in (0, 8, 16, 24))
    fine_prev = [fh[0, c] for c in range(COMPS)]
    fine_next = [fh[1, c] for c in range(COMPS)]
    wide = lambda v: [jnp.broadcast_to(w, fine_prev[0].shape) for w in v]
    ff_prev = rusanov(fine_prev, wide(split(own_up_prev, 0)), 1)
    ff_next = rusanov(wide(split(own_up_next, 0)), fine_next, 1)
    fc_prev = rusanov(prev, own_lo, 1)
    fc_next = rusanov(own_hi, nxt, 1)
    for c in range(COMPS):
        es[c : c + 1] = jnp.sum(ff_prev[c], axis=0, keepdims=True)
        es[8 + c : 9 + c] = jnp.sum(ff_next[c], axis=0, keepdims=True)
    upper_half = sub_i >= edge
    pooled_prev = dot(es[0:8], pool(by_prev, 0.25, upper_half))
    pooled_next = dot(es[8:16], pool(by_next, 0.25, ~upper_half))
    one = lax.broadcasted_iota(jnp.int32, (1, lanes), 1)
    in_prev = (one >= by_prev) & (one < by_prev + half)
    in_next = (one >= by_next) & (one < by_next + half)

    pl.when(s > 0)(up.wait_recv)
    pl.when(s < ns - 1)(down.wait_recv)
    pl.when(s == 0)(own_low.wait)
    pl.when(s == ns - 1)(own_high.wait)
    for c in range(COMPS):
        yg[c, pl.ds(0, crows, stride=2)] = gl[c]
        yg[c, pl.ds(1, crows, stride=2)] = gu[c]
    total, _, _ = side(total, [yg[c] for c in range(COMPS)], 0, sz)
    for c in range(COMPS):
        tot[c] = total[c]

    for c in range(COMPS):
        es[32 + c * crows : 32 + (c + 1) * crows] = (
            tot[c, pl.ds(0, crows, stride=2)] + tot[c, pl.ds(1, crows, stride=2)]
        )
    average = dot(es[32:], pool_own)
    for c in range(COMPS):
        low = jnp.where(in_prev, pooled_prev[c : c + 1] - fc_prev[c], 0.0)
        high = jnp.where(in_next, fc_next[c] - pooled_next[c : c + 1], 0.0)
        out = gain[c] + jnp.where(crow == 0, low, 0.0)
        out = out + jnp.where(crow == crows - 1, high, 0.0)
        gain[c] = jnp.where(covered, -average[c * crows : (c + 1) * crows], out)

    told = slots.at[pl.ds(0, count - 1)]
    pl.when(s < ns - 1)(up.wait_send)
    pl.when(s > 0)(down.wait_send)
    pltpu.make_async_copy(told, told, send_a).wait()
    pltpu.make_async_copy(told, told, recv_a).wait()
    srow = lax.broadcasted_iota(jnp.int32, slots.shape, 0)
    merged = jnp.max(jnp.where(srow < count - 1, slots[...], local), axis=0, keepdims=True)
    info[...] = jnp.broadcast_to(merged, info.shape)


def finish(u_ref, tot, base, gain, info, fo, co):
    hdt = 0.5 * (0.8 / info[0:1, :])
    for c in range(COMPS):
        fo[c] = u_ref[c] - hdt * tot[c]
        co[c] = base[c] + hdt * gain[c]


def shards(nb, ns, fine_state, coarse_state, box_y):
    layers, cells = fine_state.shape[2:]
    lanes = coarse_state.shape[3]
    crows = coarse_state.shape[2]
    blocks = cells // lanes
    rows = blocks * layers
    f4 = fine_state[0].reshape(COMPS, layers, blocks, lanes).transpose(0, 2, 1, 3)
    f2 = f4.reshape(COMPS, rows, lanes)
    c3 = coarse_state.reshape(COMPS, crows, lanes)
    f32 = lambda *shape: jax.ShapeDtypeStruct(shape, jnp.float32)
    buf = lambda *shape: pltpu.VMEM(shape, jnp.float32)
    vmem = pl.BlockSpec(memory_space=pltpu.VMEM)
    hbm = pl.BlockSpec(memory_space=pltpu.HBM)
    fine = (COMPS, rows, lanes)
    coarse = (COMPS, crows, lanes)
    dma = pltpu.SemaphoreType.DMA
    u, tot, base, gain, info = pl.pallas_call(
        functools.partial(advance, nb, ns),
        out_shape=(buf(*fine), buf(*fine), buf(*coarse), buf(*coarse), buf(8, lanes)),
        in_specs=[pl.BlockSpec(memory_space=pltpu.SMEM), hbm, hbm, hbm],
        out_specs=(vmem,) * 5,
        scratch_shapes=[
            buf(*coarse), buf(*coarse), buf(*coarse),
            buf(*coarse), buf(*coarse),
            buf(2, COMPS, lanes), buf(2, COMPS, layers, lanes),
            buf(32 + COMPS * crows, lanes), buf(*fine), buf(*fine),
            buf(1, lanes), buf(nb * ns, lanes), buf(8, lanes), buf(2, 8, lanes),
            dma, dma, dma((8,)), dma((10,)), dma((2,)), pltpu.SemaphoreType.REGULAR,
        ],
        compiler_params=pltpu.CompilerParams(collective_id=0, has_side_effects=True),
        name="advance",
    )(box_y, f4, c3, f2)
    fo, co = pl.pallas_call(
        finish,
        out_shape=(f32(*fine), f32(*coarse)),
        in_specs=[vmem] * 5,
        out_specs=(vmem, vmem),
        name="finish",
    )(*(pltpu.with_memory_space_constraint(v, pltpu.VMEM) for v in (u, tot, base, gain, info)))
    fresh = fo.reshape(COMPS, blocks, layers, lanes).transpose(0, 2, 1, 3)
    return fresh.reshape(1, COMPS, layers, cells), co.reshape(coarse_state.shape)


def solution(mesh):
    placed = (P("box", None, "sub", None), P(None, "sub", "box", None), P("box"))
    return jax.shard_map(
        functools.partial(shards, mesh.shape["box"], mesh.shape["sub"]),
        mesh=mesh,
        in_specs=placed,
        out_specs=(P("box", None, "sub", None), P(None, "sub", "box", None)),
        check_vma=False,
    )
```
